32 devices in a mesh: dp: 8 (over y, x, core), fsdp: 4 (over z).
Axes of the slice: x: 2, y: 2, z: 4, core: 2. Of those that a mesh axis runs over, the one named last changes fastest.
Arguments:
- tokens_in: bfloat16 [16384, 768], P(('dp', 'fsdp'))
- image_tokens: bfloat16 [65536, 768], P(('dp', 'fsdp'))
- out_cotangent: bfloat16 [16384, 768], P(('dp', 'fsdp')), may hold values from -6 to 6
- caption_lengths: int32 [256], P(('dp', 'fsdp')), may hold values from 1 to 64, as said below
- attn_params: float32 [4721664], P(('dp', 'fsdp'))
- attn_first: float32 [4721664], P(('dp', 'fsdp'))
- attn_second: float32 [4721664], P(('dp', 'fsdp')), as said below
- attn_average: float32 [4721664], P(('dp', 'fsdp'))
- mlp_params: float32 [4720128], P(('dp', 'fsdp'))
- mlp_first: float32 [4720128], P(('dp', 'fsdp'))
- mlp_second: float32 [4720128], P(('dp', 'fsdp')), as said below
- mlp_average: float32 [4720128], P(('dp', 'fsdp'))
- adam_step: int32 [1], replicated, may hold values from 1 to 4
- learn_rate: float32 [1], replicated, may hold values from 0.05 to 0.1
Outputs:
- block_out: bfloat16 [16384, 768], P(('dp', 'fsdp'))
- input_grad: bfloat16 [16384, 768], P(('dp', 'fsdp'))
- image_grad: bfloat16 [65536, 768], P(('dp', 'fsdp'))
- grad_norm: float32 [1], replicated
- attn_first_new: float32 [4721664], P(('dp', 'fsdp'))
- attn_second_new: float32 [4721664], P(('dp', 'fsdp'))
- attn_params_new: float32 [4721664], P(('dp', 'fsdp'))
- attn_average_new: float32 [4721664], P(('dp', 'fsdp'))
- attn_copy: bfloat16 [4721664], P(('dp', 'fsdp'))
- mlp_first_new: float32 [4720128], P(('dp', 'fsdp'))
- mlp_second_new: float32 [4720128], P(('dp', 'fsdp'))
- mlp_params_new: float32 [4720128], P(('dp', 'fsdp'))
- mlp_average_new: float32 [4720128], P(('dp', 'fsdp'))
- mlp_copy: bfloat16 [4720128], P(('dp', 'fsdp'))
The draws below stay inside these ranges and needn't reach their ends.
Inputs may be any that keep to these rules, and one draw needn't show every extreme that they name: `caption_lengths`: each device's block of 8 consecutive captions holds at least one caption of length 64. `attn_second`: every entry is positive. `mlp_second`: every entry is positive.
All inputs are finite; a program needn't handle non-finite values.
Results may differ from the reference program's by a relative error of at most 0.023.
Values may be sent and summed in bfloat16 or wider, within the bound.
No kernel may reach another device: no remote copies, remote signals or barrier semaphores. Data moves between devices by JAX's collectives and lax.ppermute only.
A program may use at most 256 MiB of HBM per device.

```python
import math
import jax
import jax.numpy as jnp
from jax import lax

D = 768
HEADS = 12
HD = 64
FF = 3072
IMG = 256
SEQ = 64
CAP_DEV = 8
CAPTIONS = 256
TOKENS = 16384
IMG_ROWS = 65536
ATT_PARAMS = 4721664
MLP_PARAMS = 4720128


def activation_draw(key, count):
    keys = jax.random.split(key, 3)
    column = jnp.arange(D) / D
    row_factor = jnp.exp(jax.random.uniform(keys[2], (count, 1), jnp.float32, math.log(0.5), math.log(2.0)))
    base = jax.random.normal(keys[0], (count, D), jnp.float32)
    rising = 3.0 ** column
    col_factor = jnp.exp(jax.random.uniform(keys[1], (D,), jnp.float32, math.log(0.35), math.log(1.1)))
    return (base * row_factor * rising * col_factor).astype(jnp.bfloat16)


def draw_tokens_in(key, part):
    return activation_draw(jax.random.fold_in(key, 3), TOKENS)


def draw_image_tokens(key, part):
    return activation_draw(jax.random.fold_in(key, 5), IMG_ROWS)


def draw_caption_lengths(key, part):
    keys = jax.random.split(jax.random.fold_in(key, 7), 3)
    blocks = CAPTIONS // CAP_DEV
    first_part = jax.random.randint(keys[0], (CAPTIONS,), 0, SEQ)
    second_part = jax.random.randint(keys[1], (CAPTIONS,), 0, 2 * SEQ)
    length = jnp.minimum(SEQ, 1 + first_part * second_part // SEQ)
    chosen = jax.random.randint(keys[2], (blocks, 1), 0, CAP_DEV)
    spot = jnp.arange(CAP_DEV)[None, :] == chosen
    return jnp.where(spot, SEQ, length.reshape(blocks, CAP_DEV)).reshape(CAPTIONS).astype(jnp.int32)


def norm_values(key, offset, count):
    keys = jax.random.split(key, 2)
    gains = jax.random.uniform(keys[0], (count,), jnp.float32, 0.7, 1.3)
    biases = 0.2 * jax.random.normal(keys[1], (count,), jnp.float32)
    return jnp.where(offset // D % 2 == 0, gains, biases)


def attn_flat(key):
    keys = jax.random.split(key, 2)
    index = jnp.arange(ATT_PARAMS)
    column = index % (8 * D)
    wider = (column >= 3 * D) & (column < 4 * D) | (column >= 7 * D)
    matrix = jax.random.normal(keys[0], (ATT_PARAMS,), jnp.float32) * jnp.where(wider, 3.0, 1.0) * D ** (-0.5)
    return jnp.where(index < 8 * D * D, matrix, norm_values(keys[1], index - 8 * D * D, ATT_PARAMS))


def mlp_flat(key):
    keys = jax.random.split(key, 2)
    index = jnp.arange(MLP_PARAMS)
    scale_entry = jnp.where(index < D * FF, D ** (-0.5), FF ** (-0.5))
    matrix = jax.random.normal(keys[0], (MLP_PARAMS,), jnp.float32) * scale_entry
    return jnp.where(index < 2 * D * FF, matrix, norm_values(keys[1], index - 2 * D * FF, MLP_PARAMS))


def clip_size():
    return (ATT_PARAMS + MLP_PARAMS) ** (-0.5)


def moment_size(count, matrix_size, group_scale):
    index = jnp.arange(count)
    base_size = group_scale * clip_size()
    return jnp.where(index < matrix_size, base_size, 3.0 * base_size)


def first_draw(key, count, matrix_size, group_scale):
    keys = jax.random.split(key, 2)
    signs = jnp.where(jax.random.bernoulli(keys[0], 0.5, (count,)), 1.0, -1.0)
    magnitude = jax.random.uniform(keys[1], (count,), jnp.float32, 0.5, 1.5)
    return 0.1 / 0.9 * moment_size(count, matrix_size, group_scale) * signs * magnitude


def second_draw(key, count, matrix_size, group_scale):
    factor = jnp.exp(jax.random.uniform(key, (count,), jnp.float32, 0.0, math.log(4.0)))
    size_entry = moment_size(count, matrix_size, group_scale)
    return 0.001 / 0.999 * size_entry * size_entry * factor


def draw_attn_params(key, part):
    return attn_flat(jax.random.fold_in(key, 21))


def draw_attn_average(key, part):
    return attn_flat(jax.random.fold_in(key, 22))


def draw_attn_first(key, part):
    return first_draw(jax.random.fold_in(key, 23), ATT_PARAMS, 8 * D * D, 1.0)


def draw_attn_second(key, part):
    return second_draw(jax.random.fold_in(key, 24), ATT_PARAMS, 8 * D * D, 1.0)


def draw_mlp_params(key, part):
    return mlp_flat(jax.random.fold_in(key, 31))


def draw_mlp_average(key, part):
    return mlp_flat(jax.random.fold_in(key, 32))


def draw_mlp_first(key, part):
    return first_draw(jax.random.fold_in(key, 33), MLP_PARAMS, 2 * D * FF, 0.25)


def draw_mlp_second(key, part):
    return second_draw(jax.random.fold_in(key, 34), MLP_PARAMS, 2 * D * FF, 0.25)


def block_levels(stream_key, extent, shards, least, largest):
    gain = 1.0
    for axis_at, shards_of in shards:
        heights = jax.random.uniform(jax.random.fold_in(jax.random.fold_in(stream_key, 6), axis_at), (shards_of,), jnp.float32, least / len(shards), largest / len(shards))
        gain = gain * jnp.repeat(jnp.exp(heights), extent[axis_at] // shards_of).reshape((-1,) + (1,) * (len(extent) - 1 - axis_at))
    return gain


def scatter_about(key, extent, scale, most, shards=(), held_as=jnp.bfloat16):
    result = scale * jax.random.normal(key, extent, jnp.float32)
    if shards:
        result = result * block_levels(key, extent, shards, -0.22, 0.18)
    return jnp.clip(result, -most, most).astype(held_as)


def setup_inputs(seed: int = 0) -> dict:
    seeds = jax.random.split(jax.random.key(seed), 15)
    return {
        "tokens_in": draw_tokens_in(jax.random.fold_in(seeds[14], 71), 0),
        "image_tokens": draw_image_tokens(jax.random.fold_in(seeds[14], 71), 0),
        "out_cotangent": scatter_about(seeds[2], (TOKENS, D), 1.0, 6.0, ((0, 32),)),
        "caption_lengths": draw_caption_lengths(jax.random.fold_in(seeds[14], 71), 0),
        "attn_params": draw_attn_params(jax.random.fold_in(seeds[14], 71), 0),
        "attn_first": draw_attn_first(jax.random.fold_in(seeds[14], 71), 0),
        "attn_second": draw_attn_second(jax.random.fold_in(seeds[14], 71), 0),
        "attn_average": draw_attn_average(jax.random.fold_in(seeds[14], 71), 0),
        "mlp_params": draw_mlp_params(jax.random.fold_in(seeds[14], 71), 0),
        "mlp_first": draw_mlp_first(jax.random.fold_in(seeds[14], 71), 0),
        "mlp_second": draw_mlp_second(jax.random.fold_in(seeds[14], 71), 0),
        "mlp_average": draw_mlp_average(jax.random.fold_in(seeds[14], 71), 0),
        "adam_step": jax.random.randint(seeds[12], (1,), 1, 5).astype(jnp.int32),
        "learn_rate": jnp.clip(jax.random.uniform(seeds[13], (1,), jnp.float32, 0.05, 0.1), 0.05, 0.1),
    }


clip_limit = 1.0

@jax.custom_vjp
def low(v):
    return lax.optimization_barrier(v.astype(jnp.bfloat16)).astype(jnp.float32)

@jax.custom_vjp
def low_back(v):
    return v

def low_keep(v):
    return (low(v), None)

def low_pass(kept, grad):
    return (grad,)

def back_keep(v):
    return (v, None)

def back_low(kept, grad):
    return (low(grad),)
low.defvjp(low_keep, low_pass)
low_back.defvjp(back_keep, back_low)

def matmul(left, right):
    return jnp.dot(left, right, precision=lax.Precision.HIGHEST, preferred_element_type=jnp.float32)

def layer_norm(rows, gain_row, bias_row):
    center = rows - lax.optimization_barrier(jnp.mean(rows, axis=-1, keepdims=True))
    spread = lax.optimization_barrier(jnp.mean(center * center, axis=-1, keepdims=True))
    return center * lax.rsqrt(spread + 1e-05) * gain_row + bias_row

def gelu_tanh(values):
    return 0.5 * values * (1.0 + jnp.tanh(0.7978845608028654 * (values + 0.044715 * values * values * values)))

def attend(queries, key_rows, value_rows, allowed):
    scores = jnp.einsum('cqhe,ckhe->chqk', queries, key_rows, precision=lax.Precision.HIGHEST) * HD ** (-0.5)
    if allowed is not None:
        scores = jnp.where(allowed[:, None], scores, -1e+30)
    scores = low_back(scores)
    top_score = lax.optimization_barrier(jnp.max(scores, axis=-1, keepdims=True))
    expo = jnp.exp(scores - top_score)
    chance = expo / lax.optimization_barrier(jnp.sum(expo, axis=-1, keepdims=True))
    return jnp.einsum('chqk,ckhe->cqhe', low(chance), value_rows, precision=lax.Precision.HIGHEST)

def unpack(attn_full, mlp_full):
    square = attn_full[:8 * D * D].reshape(D, 8 * D)
    norms_attn = attn_full[8 * D * D:].reshape(4, D)
    w_up = mlp_full[:D * FF].reshape(D, FF)
    w_down = mlp_full[D * FF:2 * D * FF].reshape(FF, D)
    norms_mlp = mlp_full[2 * D * FF:].reshape(2, D)
    return (square[:, :3 * D], square[:, 3 * D:4 * D], square[:, 4 * D:5 * D], square[:, 5 * D:7 * D], square[:, 7 * D:], norms_attn, w_up, w_down, norms_mlp)

def group_layer(weights, group):
    w_qkv, w_self, w_crossq, w_crosskv, w_crossout, norms_attn, w_up, w_down, norms_mlp = weights
    rows_x, rows_img, lengths = group
    captions = lengths.shape[0]
    position = jnp.arange(SEQ)
    valid = position[None, :] < lengths[:, None]
    allowed = (position[:, None] >= position[None, :])[None] & valid[:, None, :]
    normed_one = low(layer_norm(rows_x, norms_attn[0], norms_attn[1]))
    qkv_rows = low(low_back(matmul(normed_one, w_qkv))).reshape(captions, SEQ, 3, HEADS, HD)
    self_mix = attend(qkv_rows[:, :, 0], qkv_rows[:, :, 1], qkv_rows[:, :, 2], allowed)
    self_mix = low(low_back(self_mix.reshape(captions * SEQ, D)))
    hidden_one = rows_x + low_back(matmul(self_mix, w_self))
    normed_two = low(layer_norm(hidden_one, norms_attn[2], norms_attn[3]))
    cross_query = low(low_back(matmul(normed_two, w_crossq))).reshape(captions, SEQ, HEADS, HD)
    cross_kv = low(low_back(matmul(rows_img, w_crosskv))).reshape(captions, IMG, 2, HEADS, HD)
    cross_mix = attend(cross_query, cross_kv[:, :, 0], cross_kv[:, :, 1], None)
    cross_mix = low(low_back(cross_mix.reshape(captions * SEQ, D)))
    hidden_two = hidden_one + low_back(matmul(cross_mix, w_crossout))
    normed_three = low(layer_norm(hidden_two, norms_mlp[0], norms_mlp[1]))
    activated = low(gelu_tanh(low_back(matmul(normed_three, w_up))))
    return hidden_two + matmul(activated, w_down)

def adamw(params, first, second, average, grad, step_value, rate):
    first_new = 0.9 * first + 0.1 * grad
    second_new = 0.999 * second + 0.001 * grad * grad
    first_hat = first_new / (1.0 - jnp.power(0.9, step_value))
    second_hat = second_new / (1.0 - jnp.power(0.999, step_value))
    params_new = params - rate * (first_hat / (jnp.sqrt(second_hat) + 1e-08) + 0.01 * params)
    average_new = 0.8 * average + 0.2 * params_new
    return (first_new, second_new, params_new, average_new, params_new.astype(jnp.bfloat16))

def reference(tokens_in, image_tokens, out_cotangent, caption_lengths, attn_params, attn_first, attn_second, attn_average, mlp_params, mlp_first, mlp_second, mlp_average, adam_step, learn_rate):
    groups = CAPTIONS // CAP_DEV
    rows_x = tokens_in.astype(jnp.float32).reshape(groups, CAP_DEV * SEQ, D)
    rows_img = image_tokens.astype(jnp.float32).reshape(groups, CAP_DEV * IMG, D)
    lengths = caption_lengths.reshape(groups, CAP_DEV)
    layer_saved = jax.checkpoint(group_layer)

    def forward(attn_vec, mlp_vec, xs_all, imgs_all):
        weights = unpack(low(attn_vec), low(mlp_vec))

        def one_group(carry, group):
            return (carry, layer_saved(weights, group))
        unused, outputs = lax.scan(one_group, jnp.zeros((), jnp.float32), (xs_all, imgs_all, lengths))
        return outputs
    block, pull = jax.vjp(forward, attn_params, mlp_params, rows_x, rows_img)
    valid = (jnp.arange(SEQ)[None, :] < caption_lengths[:, None]).astype(jnp.float32)
    cotangent = out_cotangent.astype(jnp.float32).reshape(CAPTIONS, SEQ, D) * valid[:, :, None]
    attn_grad, mlp_grad, x_grad, img_grad = pull(cotangent.reshape(groups, CAP_DEV * SEQ, D))
    total = jnp.sum(attn_grad * attn_grad) + jnp.sum(mlp_grad * mlp_grad)
    grad_norm = jnp.sqrt(total)
    clip = jnp.minimum(1.0, clip_limit / (grad_norm + 1e-06))
    step_value = adam_step[0].astype(jnp.float32)
    rate = learn_rate[0]
    attn_new = adamw(attn_params, attn_first, attn_second, attn_average, attn_grad * clip, step_value, rate)
    mlp_new = adamw(mlp_params, mlp_first, mlp_second, mlp_average, mlp_grad * clip, step_value, rate)
    return (block.reshape(TOKENS, D).astype(jnp.bfloat16), x_grad.reshape(TOKENS, D).astype(jnp.bfloat16), img_grad.reshape(IMG_ROWS, D).astype(jnp.bfloat16), grad_norm.reshape(1), attn_new[0], attn_new[1], attn_new[2], attn_new[3], attn_new[4], mlp_new[0], mlp_new[1], mlp_new[2], mlp_new[3], mlp_new[4])
```

```python
import jax
import jax.numpy as jnp
from jax import lax
from jax.sharding import PartitionSpec as P

D = 768
HEADS = 12
HD = 64
FF = 3072
IMG = 256
SEQ = 64
AXES = ("dp", "fsdp")
NORMS = 6 * D


clip_limit = 1.0


def layer_norm(rows, gain_row, bias_row):
    center = rows - jnp.mean(rows, axis=-1, keepdims=True)
    spread = jnp.mean(center * center, axis=-1, keepdims=True)
    return center * lax.rsqrt(spread + 1e-05) * gain_row + bias_row


def gelu_tanh(values):
    return (
        0.5
        * values
        * (1.0 + jnp.tanh(0.7978845608028654 * (values + 0.044715 * values * values * values)))
    )


def norm_back(rows, gain_row, bias_row, d_normed):
    unused, pull = jax.vjp(
        layer_norm, rows, gain_row.astype(jnp.float32), bias_row.astype(jnp.float32)
    )
    return pull(d_normed)


def product(form, left, right):
    return jnp.einsum(form, left, right, preferred_element_type=jnp.float32)


def round_up(count, step):
    return -(-count // step) * step


def device_count():
    return lax.axis_size(AXES)


def own_index():
    return lax.axis_index(AXES)


def next_pairs(count):
    return [(i, i + 1) for i in range(count - 1)]


def prior_pairs(count):
    return [(i + 1, i) for i in range(count - 1)]


def align_shard(flat_vec, tail):
    count = device_count()
    step = tail // count
    size = flat_vec.shape[0] - step
    low = flat_vec.astype(jnp.bfloat16)
    ending = low[flat_vec.shape[0] - tail :]
    before = lax.ppermute(ending, AXES, next_pairs(count))
    both = jnp.concatenate([before, low])
    block = lax.dynamic_slice(both, (tail - step * own_index(),), (size,))
    return block, ending


def unalign_shard(block, ending, tail):
    count = device_count()
    step = tail // count
    index = own_index()
    after = lax.ppermute(block[:tail], AXES, prior_pairs(count))
    after = jnp.where(index == count - 1, ending, after)
    both = jnp.concatenate([block, after])
    return lax.dynamic_slice(both, (step * index,), (block.shape[0] + step,))


def gather_weights(attn_params, mlp_params):
    count = device_count()
    rows = D // count
    width = round_up(NORMS // rows, 128)
    attn_block, attn_end = align_shard(attn_params, 4 * D)
    mlp_block, mlp_end = align_shard(mlp_params, 2 * D)
    norms = jnp.concatenate(
        [attn_end, mlp_end, jnp.zeros((rows * width - NORMS,), jnp.bfloat16)]
    )
    attn_rows = jnp.concatenate(
        [attn_block.reshape(rows, 8 * D), norms.reshape(rows, width)], axis=1
    )
    half = count // 2
    up_rows = D // half
    as_up = mlp_block.reshape(up_rows, 4, D).swapaxes(0, 1)
    as_down = mlp_block.reshape(4, up_rows, D)
    mlp_rows = jnp.where(own_index() < half, as_up, as_down)
    square = lax.all_gather(attn_rows, AXES, axis=0, tiled=True)
    stack = lax.all_gather(mlp_rows, AXES, axis=0, tiled=True)
    stack = stack.reshape(2, half, 4, up_rows, D)
    w_up = stack[0].swapaxes(1, 2).reshape(D, FF)
    w_down = stack[1].reshape(FF, D)
    vectors = square[D - rows :, 8 * D :].reshape(-1)
    return (
        square[:, : 3 * D],
        square[:, 3 * D : 4 * D],
        square[:, 4 * D : 5 * D],
        square[:, 5 * D : 7 * D],
        square[:, 7 * D : 8 * D],
        vectors[: 4 * D].reshape(4, D),
        w_up,
        w_down,
        vectors[4 * D : 6 * D].reshape(2, D),
    )


def scatter_sum(full):
    part = lax.psum_scatter(full, "dp", scatter_dimension=0, tiled=True)
    return lax.psum_scatter(part, "fsdp", scatter_dimension=0, tiled=True)


def reduce_mlp(grad_up, grad_down):
    count = device_count()
    half = count // 2
    up_rows = D // half
    up_part = grad_up.reshape(half, up_rows, 4, D).swapaxes(1, 2).reshape(FF, D)
    summed = scatter_sum(jnp.concatenate([up_part, grad_down], axis=0))
    summed = summed.reshape(4, up_rows, D)
    return jnp.where(
        own_index() < half, summed.swapaxes(0, 1).reshape(-1), summed.reshape(-1)
    ).astype(jnp.float32)


def reduce_attn(parts, norm_grads):
    rows = D // device_count()
    width = round_up(NORMS // rows, 128)
    norms = jnp.concatenate(
        [norm_grads.reshape(-1), jnp.zeros((rows * width - NORMS,), jnp.float32)]
    ).reshape(rows, width)
    norms = jnp.pad(norms, ((D - rows, 0), (0, 0))).astype(jnp.bfloat16)
    summed = scatter_sum(jnp.concatenate(list(parts) + [norms], axis=1)).astype(jnp.float32)
    return summed[:, : 8 * D].reshape(-1), summed[:, 8 * D :].reshape(-1)[:NORMS]


def sum_everywhere(value):
    count = device_count()
    row = jnp.broadcast_to(value.reshape(1, 1), (count, 128))
    return jnp.sum(lax.all_to_all(row, AXES, split_axis=0, concat_axis=0, tiled=True)[:, 0])


def scores_of(queries, key_rows, allowed):
    scores = product("cqhe,ckhe->chqk", queries, key_rows) * HD ** (-0.5)
    if allowed is not None:
        scores = jnp.where(allowed[:, None], scores, -1e30)
    return scores


def attend_forward(queries, key_rows, value_rows, allowed):
    scores = scores_of(queries, key_rows, allowed)
    top_score = jnp.max(scores, axis=-1, keepdims=True)
    expo = jnp.exp(scores - top_score)
    total = jnp.sum(expo, axis=-1, keepdims=True)
    chance = (expo / total).astype(jnp.bfloat16)
    mixed = product("chqk,ckhe->cqhe", chance, value_rows)
    return (mixed, top_score + jnp.log(total))


def attend_backward(queries, key_rows, value_rows, allowed, log_total, d_mixed):
    scores = scores_of(queries, key_rows, allowed)
    chance = jnp.exp(scores - log_total)
    d_values = product("chqk,cqhe->ckhe", chance.astype(jnp.bfloat16), d_mixed)
    d_chance = product("cqhe,ckhe->chqk", d_mixed, value_rows)
    d_scores = (chance * (d_chance - jnp.sum(chance * d_chance, axis=-1, keepdims=True))).astype(
        jnp.bfloat16
    )
    d_queries = product("chqk,ckhe->cqhe", d_scores, key_rows) * HD ** (-0.5)
    d_keys = product("chqk,cqhe->ckhe", d_scores, queries) * HD ** (-0.5)
    return (d_queries, d_keys, d_values)


def adamw(params, first, second, average, grad, step_value, rate):
    first_new = 0.9 * first + 0.1 * grad
    second_new = 0.999 * second + 0.001 * grad * grad
    first_hat = first_new / (1.0 - jnp.power(0.9, step_value))
    second_hat = second_new / (1.0 - jnp.power(0.999, step_value))
    params_new = params - rate * (first_hat / (jnp.sqrt(second_hat) + 1e-08) + 0.01 * params)
    average_new = 0.8 * average + 0.2 * params_new
    return (first_new, second_new, params_new, average_new, params_new.astype(jnp.bfloat16))


def shards(
    tokens_in,
    image_tokens,
    out_cotangent,
    caption_lengths,
    attn_params,
    attn_first,
    attn_second,
    attn_average,
    mlp_params,
    mlp_first,
    mlp_second,
    mlp_average,
    adam_step,
    learn_rate,
):
    w_qkv, w_self, w_crossq, w_crosskv, w_crossout, norms_attn, w_up, w_down, norms_mlp = (
        gather_weights(attn_params, mlp_params)
    )
    captions = caption_lengths.shape[0]
    position = jnp.arange(SEQ)
    valid = position[None, :] < caption_lengths[:, None]
    allowed = (position[:, None] >= position[None, :])[None] & valid[:, None, :]
    rows_x = tokens_in.astype(jnp.float32)
    normed_one = layer_norm(rows_x, norms_attn[0], norms_attn[1]).astype(jnp.bfloat16)
    qkv_rows = (
        jnp.dot(normed_one, w_qkv, preferred_element_type=jnp.float32)
        .astype(jnp.bfloat16)
        .reshape(captions, SEQ, 3, HEADS, HD)
    )
    self_mix, self_lse = attend_forward(
        qkv_rows[:, :, 0], qkv_rows[:, :, 1], qkv_rows[:, :, 2], allowed
    )
    self_mix = self_mix.reshape(captions * SEQ, D).astype(jnp.bfloat16)
    hidden_one = rows_x + jnp.dot(self_mix, w_self, preferred_element_type=jnp.float32)
    normed_two = layer_norm(hidden_one, norms_attn[2], norms_attn[3]).astype(jnp.bfloat16)
    cross_query = (
        jnp.dot(normed_two, w_crossq, preferred_element_type=jnp.float32)
        .astype(jnp.bfloat16)
        .reshape(captions, SEQ, HEADS, HD)
    )
    cross_kv = (
        jnp.dot(image_tokens, w_crosskv, preferred_element_type=jnp.float32)
        .astype(jnp.bfloat16)
        .reshape(captions, IMG, 2, HEADS, HD)
    )
    cross_mix, cross_lse = attend_forward(cross_query, cross_kv[:, :, 0], cross_kv[:, :, 1], None)
    cross_mix = cross_mix.reshape(captions * SEQ, D).astype(jnp.bfloat16)
    hidden_two = hidden_one + jnp.dot(cross_mix, w_crossout, preferred_element_type=jnp.float32)
    normed_three = layer_norm(hidden_two, norms_mlp[0], norms_mlp[1]).astype(jnp.bfloat16)
    up_rows = jnp.dot(normed_three, w_up, preferred_element_type=jnp.float32)
    activated = gelu_tanh(up_rows).astype(jnp.bfloat16)
    block_out = (
        hidden_two + jnp.dot(activated, w_down, preferred_element_type=jnp.float32)
    ).astype(jnp.bfloat16)
    valid_rows = valid.reshape(captions * SEQ, 1)
    d_out = jnp.where(valid_rows, out_cotangent, jnp.zeros((), jnp.bfloat16))
    grad_down = product("tf,td->fd", activated, d_out)
    d_act = product("td,fd->tf", d_out, w_down)
    unused_up, gelu_pull = jax.vjp(gelu_tanh, up_rows)
    d_up = gelu_pull(d_act)[0].astype(jnp.bfloat16)
    grad_up = product("td,tf->df", normed_three, d_up)
    d_normed_three = product("tf,df->td", d_up, w_up)
    d_hidden_two, grad_gain_three, grad_bias_three = norm_back(
        hidden_two, norms_mlp[0], norms_mlp[1], d_normed_three
    )
    d_hidden_two = d_hidden_two + d_out.astype(jnp.float32)
    mlp_block = reduce_mlp(grad_up.astype(jnp.bfloat16), grad_down.astype(jnp.bfloat16))
    d_two_low = d_hidden_two.astype(jnp.bfloat16)
    grad_crossout = product("tf,td->fd", cross_mix, d_two_low)
    d_cross_mix = (
        product("td,fd->tf", d_two_low, w_crossout)
        .astype(jnp.bfloat16)
        .reshape(captions, SEQ, HEADS, HD)
    )
    d_query, d_key, d_value = attend_backward(
        cross_query, cross_kv[:, :, 0], cross_kv[:, :, 1], None, cross_lse, d_cross_mix
    )
    d_cross_query = d_query.astype(jnp.bfloat16).reshape(captions * SEQ, D)
    d_cross_kv = (
        jnp.stack([d_key, d_value], axis=2).astype(jnp.bfloat16).reshape(captions * IMG, 2 * D)
    )
    grad_crossq = product("td,tf->df", normed_two, d_cross_query)
    grad_crosskv = product("td,tf->df", image_tokens, d_cross_kv)
    image_grad = product("tf,df->td", d_cross_kv, w_crosskv).astype(jnp.bfloat16)
    d_normed_two = product("tf,df->td", d_cross_query, w_crossq)
    d_hidden_one, grad_gain_two, grad_bias_two = norm_back(
        hidden_one, norms_attn[2], norms_attn[3], d_normed_two
    )
    d_hidden_one = d_hidden_one + d_hidden_two
    d_one_low = d_hidden_one.astype(jnp.bfloat16)
    grad_self = product("tf,td->fd", self_mix, d_one_low)
    d_self_mix = (
        product("td,fd->tf", d_one_low, w_self)
        .astype(jnp.bfloat16)
        .reshape(captions, SEQ, HEADS, HD)
    )
    d_query, d_key, d_value = attend_backward(
        qkv_rows[:, :, 0], qkv_rows[:, :, 1], qkv_rows[:, :, 2], allowed, self_lse, d_self_mix
    )
    d_qkv = (
        jnp.stack([d_query, d_key, d_value], axis=2)
        .astype(jnp.bfloat16)
        .reshape(captions * SEQ, 3 * D)
    )
    grad_qkv = product("td,tf->df", normed_one, d_qkv)
    d_normed_one = product("tf,df->td", d_qkv, w_qkv)
    d_rows, grad_gain_one, grad_bias_one = norm_back(
        rows_x, norms_attn[0], norms_attn[1], d_normed_one
    )
    input_grad = (d_rows + d_hidden_one).astype(jnp.bfloat16)
    attn_block, norm_block = reduce_attn(
        [
            grad.astype(jnp.bfloat16)
            for grad in (grad_qkv, grad_self, grad_crossq, grad_crosskv, grad_crossout)
        ],
        jnp.stack(
            [
                grad_gain_one,
                grad_bias_one,
                grad_gain_two,
                grad_bias_two,
                grad_gain_three,
                grad_bias_three,
            ]
        ),
    )
    local_squares = (
        jnp.sum(attn_block * attn_block)
        + jnp.sum(mlp_block * mlp_block)
        + jnp.sum(norm_block * norm_block)
    )
    grad_norm = jnp.sqrt(sum_everywhere(local_squares))
    attn_grad = unalign_shard(attn_block, norm_block[: 4 * D], 4 * D)
    mlp_grad = unalign_shard(mlp_block, norm_block[4 * D :], 2 * D)
    clip = jnp.minimum(1.0, clip_limit / (grad_norm + 1e-06))
    step_value = adam_step[0].astype(jnp.float32)
    rate = learn_rate[0]
    attn_new = adamw(
        attn_params, attn_first, attn_second, attn_average, attn_grad * clip, step_value, rate
    )
    mlp_new = adamw(
        mlp_params, mlp_first, mlp_second, mlp_average, mlp_grad * clip, step_value, rate
    )
    return (
        block_out,
        input_grad,
        image_grad,
        grad_norm.reshape(1),
        attn_new[0],
        attn_new[1],
        attn_new[2],
        attn_new[3],
        attn_new[4],
        mlp_new[0],
        mlp_new[1],
        mlp_new[2],
        mlp_new[3],
        mlp_new[4],
    )


def solution(mesh):
    return jax.shard_map(
        shards,
        mesh=mesh,
        in_specs=(
            P(("dp", "fsdp"), None),
            P(("dp", "fsdp"), None),
            P(("dp", "fsdp"), None),
            P(("dp", "fsdp")),
            P(("dp", "fsdp")),
            P(("dp", "fsdp")),
            P(("dp", "fsdp")),
            P(("dp", "fsdp")),
            P(("dp", "fsdp")),
            P(("dp", "fsdp")),
            P(("dp", "fsdp")),
            P(("dp", "fsdp")),
            P(),
            P(),
        ),
        out_specs=(
            P(("dp", "fsdp"), None),
            P(("dp", "fsdp"), None),
            P(("dp", "fsdp"), None),
            P(),
            P(("dp", "fsdp")),
            P(("dp", "fsdp")),
            P(("dp", "fsdp")),
            P(("dp", "fsdp")),
            P(("dp", "fsdp")),
            P(("dp", "fsdp")),
            P(("dp", "fsdp")),
            P(("dp", "fsdp")),
            P(("dp", "fsdp")),
            P(("dp", "fsdp")),
        ),
        check_vma=False,
    )
```
